32 devices in a mesh: wide: 8 (over z, y), narrow: 4 (over x, core).
Axes of the slice: x: 2, y: 2, z: 4, core: 2. Of those that a mesh axis runs over, the one named last changes fastest.
Arguments:
- left_emb: float32 [8, 256, 256], P('wide', 'narrow'), may hold values from -1.5 to 1.5
- left_acc: float32 [8, 256], P('wide', 'narrow'), may hold values from 0.01 to 1
- right_emb: float32 [8, 256, 256], P('wide', 'narrow'), may hold values from -1.5 to 1.5
- right_acc: float32 [8, 256], P('wide', 'narrow'), may hold values from 0.01 to 1
- operators: float32 [8, 256, 256], replicated, may hold values from -0.375 to 0.375
- op_acc: float32 [8, 256], replicated, may hold values from 10 to 1000
- edge_left: int32 [8, 4, 512], P('wide', 'narrow'), may hold values from 0 to 255
- edge_right: int32 [8, 4, 512], P('wide', 'narrow'), may hold values from 0 to 255
- negatives: int32 [8, 4, 1024], P('wide', 'narrow'), may hold values from 0 to 255
- group_relation: int32 [8, 4], P('wide', 'narrow'), may hold values from 0 to 7
Outputs:
- left_new: float32 [8, 256, 256], P('wide', 'narrow')
- left_acc_new: float32 [8, 256], P('wide', 'narrow')
- right_next: float32 [8, 256, 256], P('wide', 'narrow')
- right_acc_next: float32 [8, 256], P('wide', 'narrow')
- operators_new: float32 [8, 256, 256], replicated
- op_acc_new: float32 [8, 256], replicated
The draws below stay inside these ranges and needn't reach their ends.
All inputs are finite; a program needn't handle non-finite values.
Results may differ from the reference program's by a relative error of at most 0.0003.
Values sent between devices are 32-bit elements; how exact they have to be, the bound alone decides.
A program may use at most 64 MiB of HBM per device.

```python
import math
import jax
import jax.numpy as jnp
import numpy as np
from jax import lax

D = 256
REL = 8
E_DEV = 512
NEG = 1024
PART = 256
N_WIDE = 8
N_NARROW = 4


def touch_ends(entries, stream_key, smallest, top_value):
    longest = entries.shape.index(max(entries.shape))
    spots = []
    for shift in (0, 1):
        where = [jax.random.randint(jax.random.fold_in(stream_key, axis), (), 0, length) for axis, length in enumerate(entries.shape)]
        where[longest] = (where[longest] + shift) % entries.shape[longest]
        spots.append(tuple(where))
    return entries.at[spots[0]].set(smallest).at[spots[1]].set(top_value)


def steps_of(own_key, extent, pieces, low, high):
    gain = 1.0
    for dim, blocks in pieces:
        steps = jax.random.uniform(jax.random.fold_in(jax.random.fold_in(own_key, 6), dim), (blocks,), jnp.float32, low / len(pieces), high / len(pieces))
        gain = gain * jnp.repeat(jnp.exp(steps), extent[dim] // blocks).reshape((-1,) + (1,) * (len(extent) - 1 - dim))
    return gain


def rank_table(count, lean):
    weights = [(1 << 20) // math.isqrt(rank ** lean) + 1 for rank in range(1, count + 1)]
    spread = 1 + sum(weights) // (1 << 30)
    return np.cumsum(np.array([max(1, weight // spread) for weight in weights]))


def skewed_ids(stream_key, extent, number_of, slope):
    table = rank_table(number_of, slope)
    lot = jax.random.randint(jax.random.fold_in(stream_key, 1), extent, 0, int(table[number_of - 1]))
    grade = jnp.searchsorted(jnp.asarray(table, jnp.int32), lot, side="right")
    return jax.random.permutation(jax.random.fold_in(stream_key, 2), number_of)[grade].astype(jnp.int32)


def normal_values(stream_key, dims, spread, limit, split=(), kind=jnp.bfloat16):
    gain = steps_of(stream_key, dims, split, -0.22, 0.18) if split else 1.0
    drawn = jax.random.normal(stream_key, dims, jnp.float32) * spread * gain
    return jnp.minimum(jnp.maximum(drawn, -limit), limit).astype(kind)


def setup_inputs(seed: int = 0) -> dict:
    keys = jax.random.split(jax.random.key(seed), 11)
    left_emb = normal_values(keys[0], (N_WIDE, PART, D), 0.25, 1.5, ((0, 8), (1, 4)), jnp.float32)
    left_acc = jnp.clip(jnp.exp(math.log(1.0) - 4.6051702 * jax.random.uniform(keys[1], (N_WIDE, PART), jnp.float32) ** steps_of(keys[1], (N_WIDE, PART), ((0, 8), (1, 4)), -0.2, 0.2)), 0.01, 1.0)
    right_emb = normal_values(keys[2], (N_WIDE, PART, D), 0.25, 1.5, ((0, 8), (1, 4)), jnp.float32)
    right_acc = jnp.clip(jnp.exp(math.log(1.0) - 4.6051702 * jax.random.uniform(keys[3], (N_WIDE, PART), jnp.float32) ** steps_of(keys[3], (N_WIDE, PART), ((0, 8), (1, 4)), -0.2, 0.2)), 0.01, 1.0)
    operators = normal_values(keys[4], (REL, D, D), D ** -0.5, 0.375, (), jnp.float32)
    op_acc = jnp.clip(jnp.exp(jax.random.uniform(keys[5], (REL, D), jnp.float32, math.log(10.0), math.log(1000.0))), 10.0, 1000.0)
    edge_left = touch_ends(skewed_ids(keys[6], (N_WIDE, N_NARROW, E_DEV), PART, 2), jax.random.fold_in(keys[6], 3), 0, PART - 1).astype(jnp.int32)
    edge_right = touch_ends(jax.random.randint(keys[7], (N_WIDE, N_NARROW, E_DEV), 0, PART), jax.random.fold_in(keys[7], 1), 0, PART - 1).astype(jnp.int32)
    negatives = touch_ends(jax.random.randint(keys[8], (N_WIDE, N_NARROW, NEG), 0, PART), jax.random.fold_in(keys[8], 1), 0, PART - 1).astype(jnp.int32)
    group_relation = touch_ends(skewed_ids(keys[9], (N_WIDE, N_NARROW), REL, 2), jax.random.fold_in(keys[9], 3), 0, REL - 1).astype(jnp.int32)
    return {"left_emb": left_emb, "left_acc": left_acc, "right_emb": right_emb, "right_acc": right_acc, "operators": operators, "op_acc": op_acc, "edge_left": edge_left, "edge_right": edge_right, "negatives": negatives, "group_relation": group_relation}


HI = lax.Precision.HIGHEST

def group_terms(left_rows, right_rows, neg_rows, rel_op):
    t = jnp.dot(left_rows, rel_op, precision=HI)
    pos = lax.optimization_barrier(jnp.sum(t * right_rows, axis=-1))
    neg = jnp.dot(t, neg_rows.T, precision=HI)
    gpos = -jax.nn.sigmoid(-pos)
    gneg = jax.nn.sigmoid(neg) / neg_rows.shape[0]
    grad_t = gpos[:, None] * right_rows + jnp.dot(gneg, neg_rows, precision=HI)
    grad_left = jnp.dot(grad_t, rel_op.T, precision=HI)
    grad_right = gpos[:, None] * t
    grad_neg = jnp.dot(gneg.T, t, precision=HI)
    grad_op = jnp.dot(left_rows.T, grad_t, precision=HI)
    return (grad_left, grad_right, grad_neg, grad_op)

def adagrad(param, accum, grad):
    accum_new = accum + lax.optimization_barrier(jnp.mean(grad * grad, axis=-1))
    return (param - 0.1 * grad / (jnp.sqrt(accum_new)[..., None] + 1e-08), accum_new)

def reference(left_emb, left_acc, right_emb, right_acc, operators, op_acc, edge_left, edge_right, negatives, group_relation):
    op_total = jnp.zeros(operators.shape, jnp.float32)
    lefts, laccs, rights, raccs = ([], [], [], [])
    for w in range(N_WIDE):
        lpart = left_emb[w]
        rpart = right_emb[w]

        def one(carry, n):
            gl, gr, gop = carry
            lid = edge_left[w][n]
            rid = edge_right[w][n]
            nid = negatives[w][n]
            rel = group_relation[w][n]
            rel_op = lax.dynamic_index_in_dim(operators, rel, 0, keepdims=False)
            dl, dr, dq, dm = group_terms(jnp.take(lpart, lid, axis=0), jnp.take(rpart, rid, axis=0), jnp.take(rpart, nid, axis=0), rel_op)
            gl = gl + jax.ops.segment_sum(dl, lid, num_segments=PART)
            gr = gr + jax.ops.segment_sum(jnp.concatenate([dr, dq], 0), jnp.concatenate([rid, nid], 0).astype(jnp.int32), num_segments=PART)
            pick = (jnp.arange(REL, dtype=jnp.int32) == rel).astype(jnp.float32)
            gop = gop + pick[:, None, None] * dm[None]
            return ((gl, gr, gop), None)
        zero_rows = jnp.zeros((PART, D), jnp.float32)
        (gl, gr, gop), unused = lax.scan(one, (zero_rows, zero_rows, jnp.zeros(operators.shape, jnp.float32)), jnp.arange(N_NARROW, dtype=jnp.int32))
        op_total = op_total + gop
        new_left, new_lacc = adagrad(lpart, left_acc[w], gl)
        new_right, new_racc = adagrad(rpart, right_acc[w], gr)
        lefts.append(new_left)
        laccs.append(new_lacc)
        rights.append(new_right)
        raccs.append(new_racc)
    ops_new, opacc_new = adagrad(operators, op_acc, op_total)
    right_all = jnp.roll(jnp.stack(rights), N_WIDE // 2, axis=0)
    racc_all = jnp.roll(jnp.stack(raccs), N_WIDE // 2, axis=0)
    return (jnp.stack(lefts), jnp.stack(laccs), right_all, racc_all, ops_new, opacc_new)
```

```python
import functools
import jax
import jax.numpy as jnp
from jax import lax
from jax.experimental import pallas as pl
from jax.experimental.pallas import tpu as pltpu
from jax.sharding import PartitionSpec as P

HI = lax.Precision.HIGHEST
MESH = pl.DeviceIdType.MESH
F32 = jnp.float32
BF16 = jnp.bfloat16
VMEM_LIMIT = 32000 * 1024
LANES = 128


def from_behind(value, axis, steps):
    count = lax.axis_size(axis)
    pairs = [(source, (source + steps) % count) for source in range(count)]
    return lax.ppermute(value, axis, pairs)


def group_terms(left_rows, right_rows, neg_rows, rel_op):
    t = jnp.dot(left_rows, rel_op, precision=HI)
    pos = jnp.sum(t * right_rows, axis=-1)
    neg = jnp.dot(t, neg_rows.T, precision=HI)
    gpos = -jax.nn.sigmoid(-pos)
    gneg = jax.nn.sigmoid(neg) / neg_rows.shape[0]
    grad_t = gpos[:, None] * right_rows + jnp.dot(gneg, neg_rows, precision=HI)
    grad_left = jnp.dot(grad_t, rel_op.T, precision=HI)
    grad_right = gpos[:, None] * t
    grad_neg = jnp.dot(gneg.T, t, precision=HI)
    grad_op = jnp.dot(left_rows.T, grad_t, precision=HI)
    return (grad_left, grad_right, grad_neg, grad_op)


def adagrad(param, accum, grad):
    accum_new = accum + jnp.mean(grad * grad, axis=-1)
    return (param - 0.1 * grad / (jnp.sqrt(accum_new)[..., None] + 1e-08), accum_new)


def rows_within(terms, ids, count):
    inside = (ids >= 0) & (ids < count)
    target = jnp.where(inside, ids, count)
    return jax.ops.segment_sum(terms, target, num_segments=count + 1)[:count]


def plain_device(
    left_emb,
    left_acc,
    right_emb,
    right_acc,
    operators,
    op_acc,
    edge_left,
    edge_right,
    negatives,
    group_relation,
):
    whole_left, whole_right = (
        lax.all_gather(left_emb, "narrow", axis=1, tiled=True),
        lax.all_gather(right_emb, "narrow", axis=1, tiled=True),
    )
    lid = edge_left[0, 0]
    rid = edge_right[0, 0]
    nid = negatives[0, 0]
    rel = group_relation[0, 0]
    rel_op = lax.dynamic_index_in_dim(operators, rel, 0, keepdims=False)
    dl, dr, dq, dm = group_terms(
        jnp.take(whole_left[0], lid, axis=0),
        jnp.take(whole_right[0], rid, axis=0),
        jnp.take(whole_right[0], nid, axis=0),
        rel_op,
    )
    right_ids = jnp.concatenate([rid, nid], 0)
    right_terms = jnp.concatenate([dr, dq], 0)
    rows = left_emb.shape[1]
    width = left_emb.shape[2]
    grads = lax.psum_scatter(
        jnp.concatenate(
            [
                rows_within(dl, lid, lax.axis_size("narrow") * rows),
                rows_within(right_terms, right_ids, lax.axis_size("narrow") * rows),
            ],
            1,
        ),
        "narrow",
        scatter_dimension=0,
        tiled=True,
    )
    new_left, new_lacc = adagrad(left_emb[0], left_acc[0], grads[:, :width])
    new_right, new_racc = adagrad(right_emb[0], right_acc[0], grads[:, width:])
    pick = (jnp.arange(operators.shape[0], dtype=jnp.int32) == rel).astype(jnp.float32)
    op_term = pick[:, None, None] * dm[None]
    op_total = lax.psum(op_term, ("wide", "narrow"))
    ops_new, opacc_new = adagrad(operators, op_acc, op_total)
    moved_right, moved_racc = from_behind((new_right, new_racc), "wide", lax.axis_size("wide") // 2)
    return (new_left[None], new_lacc[None], moved_right[None], moved_racc[None], ops_new, opacc_new)


def flip(index, d):
    out = 0
    bit = 1
    total = 0
    while bit <= d:
        here = (index // bit) % 2
        if d & bit:
            out = out + (1 - here) * bit
        else:
            out = out + here * bit
        total += bit
        bit *= 2
    return (index // bit) * bit + out if d else index


def halves(a):
    hi = a.astype(BF16)
    return hi, (a - hi.astype(F32)).astype(BF16)


def dot3(a, b, rhs_t=False):
    (ah, al), (bh, bl) = a, b
    dims = (((1,), (1 if rhs_t else 0,)), ((), ()))
    f = lambda u, v: lax.dot_general(u, v, dims, preferred_element_type=F32)
    return f(ah, bh) + (f(ah, bl) + f(al, bh))


def to_column(row):
    n = row.shape[1]
    eye = lax.broadcasted_iota(jnp.int32, (n, n), 0) == lax.broadcasted_iota(jnp.int32, (n, n), 1)
    return jnp.sum(jnp.where(eye, row, 0.0), axis=1, keepdims=True)


def to_row(column):
    n = column.shape[0]
    eye = lax.broadcasted_iota(jnp.int32, (n, n), 0) == lax.broadcasted_iota(jnp.int32, (n, n), 1)
    return jnp.sum(jnp.where(eye, column, 0.0), axis=0, keepdims=True)


def kernel(
    NW,
    NN,
    left,
    lacc_hbm,
    right,
    racc_hbm,
    ops_hbm,
    opacc_hbm,
    lids_hbm,
    rids_hbm,
    nids_hbm,
    rel_ref,
    left_out,
    lacc_out,
    right_out,
    racc_out,
    ops_out,
    opacc_out,
    lacc,
    racc,
    opacc,
    lids,
    rids,
    nids,
    left_v,
    lacc_v,
    racc_v,
    opacc_v,
    ops_v,
    wl,
    wr,
    tagb,
    accb,
    dm,
    glb,
    grb,
    near_l,
    near_r,
    far_ls,
    far_rs,
    far_l,
    far_r,
    rsb,
    part_s,
    part_r,
    own_v,
    in_sem,
    res_sem,
    out_sem,
    here_sem,
    g_send,
    g_recv,
    t_send,
    t_recv,
    s_send,
    s_recv,
    q_send,
    q_recv,
    p_send,
    p_recv,
    c_send,
    c_recv,
    a_send,
    a_recv,
):
    rows, width = left.shape[1], left.shape[2]
    part = NN * rows
    rels = ops_v.shape[0]
    q = own_v.shape[1]
    hr = rels // 2
    NZ = NW // 2
    devices = NW * NN
    lanes = accb.shape[2]
    w = lax.axis_index("wide")
    n = lax.axis_index("narrow")
    z, y = w // 2, w % 2
    x, c = n // 2, n % 2
    j = n * NW + w
    near, far = flip(n, 1), flip(n, 2)

    def rcopy(src, dst, ss, rs, to_w, to_n):
        cp = pltpu.make_async_remote_copy(
            src_ref=src,
            dst_ref=dst,
            send_sem=ss,
            recv_sem=rs,
            device_id=(to_w, to_n),
            device_id_type=MESH,
        )
        cp.start()
        return cp

    def take(ref, sem):
        pltpu.make_async_copy(ref, ref, sem).wait()

    loads = {}

    def load(name, src, dst):
        cp = pltpu.make_async_copy(src, dst, in_sem.at[len(loads)])
        cp.start()
        loads[name] = cp

    load("l", lids_hbm, lids)
    load("r", rids_hbm, rids)
    load("n", nids_hbm, nids)
    load("left", left.at[0], wl.at[n])
    load("right", right.at[0], wr.at[n])
    load("lacc", lacc_hbm, lacc)
    load("racc", racc_hbm, racc)
    load("opacc", opacc_hbm, opacc)
    load("ops", ops_hbm, ops_v)

    barrier = pltpu.get_barrier_semaphore()
    for d in range(1, NN):
        pl.semaphore_signal(barrier, inc=1, device_id=(w, flip(n, d)), device_id_type=MESH)
    for d in range(1, NW):
        pl.semaphore_signal(barrier, inc=1, device_id=(flip(w, d), n), device_id_type=MESH)
    pl.semaphore_wait(barrier, NN + NW - 2)

    rcopy(left.at[0], wl.at[n], g_send, g_recv.at[0], w, far)
    rcopy(right.at[0], wr.at[n], g_send, g_recv.at[1], w, far)
    rcopy(left.at[0], wl.at[n], g_send, g_recv.at[2], w, near)
    rcopy(right.at[0], wr.at[n], g_send, g_recv.at[3], w, near)
    for d in range(1, NN):
        pl.semaphore_signal(here_sem, inc=1, device_id=(w, flip(n, d)), device_id_type=MESH)

    for name in "lrn":
        loads[name].wait()
    edges, negs = lids.shape[2], nids.shape[2]
    ohl = lax.broadcasted_iota(jnp.int32, (part, edges), 0) == lids[0]
    ohr = lax.broadcasted_iota(jnp.int32, (part, edges), 0) == rids[0]
    ohn = lax.broadcasted_iota(jnp.int32, (part, negs), 0) == nids[0]
    nt = (((1,), (1,)), ((), ()))
    ohl16 = jnp.where(ohl, 1.0, 0.0).astype(BF16)
    ohr16 = jnp.where(ohr, 1.0, 0.0).astype(BF16)
    ohn16 = jnp.where(ohn, 1.0, 0.0).astype(BF16)
    pairs = lax.dot_general(ohl16, ohr16, nt, preferred_element_type=F32)
    cl = jnp.sum(jnp.where(ohl, 1.0, 0.0), axis=1, keepdims=True)
    cn = lax.dot_general(jnp.ones((8, negs), BF16), ohn16, nt, preferred_element_type=F32)[0:1]
    weight = cl * cn

    loads["ops"].wait()
    rel = rel_ref[0, 0]
    m = halves(ops_v[rel])
    tagb[j] = jnp.broadcast_to(rel.astype(F32), tagb.shape[1:])
    pl.semaphore_wait(here_sem, NN - 1)

    order = list(range(NZ - 1, 0, -1)) + [0]
    peers = [
        (dz, dy, dn)
        for dz in order
        for dn in range(NN - 1, -1, -1)
        for dy in (1, 0)
        if dz or dy or dn
    ]

    def peer(dz, dy, dn):
        return flip(z, dz) * 2 + flip(y, dy), flip(n, dn)

    for p in peers:
        rcopy(tagb.at[j], tagb.at[j], t_send, t_recv, *peer(*p))

    take(wl.at[n], g_recv.at[0])
    rcopy(wl.at[far], wl.at[far], g_send, g_recv.at[4], w, near)
    take(wr.at[n], g_recv.at[1])
    rcopy(wr.at[far], wr.at[far], g_send, g_recv.at[5], w, near)
    loads["left"].wait()
    loads["right"].wait()
    take(wl.at[n], g_recv.at[2])
    take(wl.at[n], g_recv.at[4])
    wl_all = wl[...].reshape(part, width)
    t = dot3(halves(wl_all), m)
    th = halves(t)
    wlt = halves(wl_all.T)
    take(wr.at[n], g_recv.at[3])
    take(wr.at[n], g_recv.at[5])
    wrh = halves(wr[...].reshape(part, width))
    s = dot3(th, wrh, rhs_t=True)
    g = weight * (jax.nn.sigmoid(s) / negs) - pairs * jax.nn.sigmoid(-s)
    dt = halves(dot3(halves(g), wrh))
    dm[...] = dot3(wlt, dt)

    def slot(i, size):
        return pl.ds(pl.multiple_of(i * size, size), size)

    for dz, dy, dn in peers:
        to_w, to_n = peer(dz, dy, dn)
        rcopy(dm.at[slot(to_n * NW + to_w, q)], rsb.at[j], s_send, s_recv.at[dz], to_w, to_n)
    rsb[j] = dm[slot(j, q), :]

    grb[...] = dot3(halves(g.T), th)
    for k in range(2):
        rcopy(grb.at[slot(k * 2 + 1 - c, rows)], near_r.at[k], q_send, q_recv.at[0], w, near)
    glb[...] = dot3(dt, m, rhs_t=True)
    for k in range(2):
        rcopy(glb.at[slot(k * 2 + 1 - c, rows)], near_l.at[k], q_send, q_recv.at[1], w, near)

    take(near_r, q_recv.at[0])
    far_rs[...] = grb[slot((1 - x) * 2 + c, rows), :] + near_r[1 - x]
    rcopy(far_rs, far_r, q_send, q_recv.at[2], w, far)
    take(near_l, q_recv.at[1])
    far_ls[...] = glb[slot((1 - x) * 2 + c, rows), :] + near_l[1 - x]
    rcopy(far_ls, far_l, q_send, q_recv.at[3], w, far)

    def row_step(p, acc_row, grad):
        acc = to_column(acc_row) + jnp.sum(grad * grad, axis=1, keepdims=True) / width
        return p - 0.1 * grad / (jnp.sqrt(acc) + 1e-08), to_row(acc)

    own = slot(n, rows)
    for name in ("lacc", "racc", "opacc"):
        loads[name].wait()
    place = lax.broadcasted_iota(jnp.int32, (rels, q, width), 2) == (
        j * q + lax.broadcasted_iota(jnp.int32, (rels, q, width), 1)
    )
    old = jnp.sum(jnp.where(place, opacc[...][:, None, :], 0.0), axis=2, keepdims=True)

    take(tagb.at[0 : devices - 1], t_recv)

    def add_up(dz, total):
        for dn in range(NN):
            for dy in range(2):
                src_w, src_n = peer(dz, dy, dn)
                i = src_n * NW + src_w
                tag = jnp.broadcast_to(tagb[i], (q, lanes))
                tag = jnp.concatenate([tag] * (width // lanes), axis=1)
                term = rsb[i]
                total = [t + jnp.where(tag == k, term, 0.0) for k, t in enumerate(total)]
        return total

    total = [jnp.zeros((q, width), F32) for k in range(rels)]
    take(rsb.at[0 : 2 * NN - 1], s_recv.at[0])
    total = add_up(0, total)
    take(rsb.at[0 : 2 * NN], s_recv.at[1])
    total = add_up(1, total)
    take(far_r, q_recv.at[2])
    new_right, new_racc = row_step(wr[n], racc[...], grb[own, :] + near_r[x] + far_r[...])
    part_s[0:rows, :] = new_right
    part_s[rows : rows + 8, 0:rows] = jnp.broadcast_to(new_racc, (8, rows))
    part_s[rows : rows + 8, rows:width] = jnp.zeros((8, width - rows), F32)
    moved = rcopy(part_s, part_r, p_send, p_recv, (w + NW // 2) % NW, n)
    for dz in range(2, NZ):
        take(rsb.at[0 : 2 * NN], s_recv.at[dz])
        total = add_up(dz, total)

    gop = jnp.stack(total)
    acc = old + jnp.sum(gop * gop, axis=2, keepdims=True) / width
    own_v[...] = ops_v[:, slot(j, q), :] - 0.1 * gop / (jnp.sqrt(acc) + 1e-08)

    def at(r0, r1, i):
        return ops_out.at[r0:r1, slot(i, q), :]

    def shard(zs, ys, xs):
        return (xs * 2 + c) * NW + zs * 2 + ys

    def away(s):
        top = z // (NZ // 2)
        m_z = top * (NZ - 1 - z) + (1 - top) * z
        v = s + (s - m_z + NZ) // NZ
        return top * (NZ - 1 - v) + (1 - top) * v

    wy = z * 2 + (1 - y)
    zs = [z] + [away(s) for s in range(NZ - 1)]

    def send(src, dst, kind, z_of, to_w, to_n):
        rcopy(src, dst, a_send, a_recv.at[kind * NZ + z_of], to_w, to_n)

    def give(src, dst):
        rcopy(src, dst, a_send, a_recv.at[7 * NZ], w, near)

    def spread(src, i, z_of):
        lo, hi = at(0, hr, i), at(hr, rels, i)
        send(src.at[0:hr], lo, 1, z_of, wy, n)
        send(src.at[hr:rels], hi, 2, z_of, w, far)
        send(src.at[0:hr], lo, 3, z_of, w, far)
        send(src.at[hr:rels], hi, 4, z_of, wy, n)
        give(src, at(0, rels, i))

    def pass_on(z_of):
        lo = at(0, hr, shard(z_of, 1 - y, x))
        take(lo, a_recv.at[1 * NZ + z_of])
        send(lo, lo, 5, z_of, w, far)
        give(lo, lo)
        hi = at(hr, rels, shard(z_of, y, 1 - x))
        take(hi, a_recv.at[2 * NZ + z_of])
        send(hi, hi, 6, z_of, wy, n)
        give(hi, hi)

    def last(z_of, kind, lo_y):
        lo = at(0, hr, shard(z_of, lo_y, 1 - x))
        take(lo, a_recv.at[kind * NZ + z_of])
        give(lo, lo)
        hi = at(hr, rels, shard(z_of, 1 - y, x if kind == 3 else 1 - x))
        take(hi, a_recv.at[(kind + 1) * NZ + z_of])
        give(hi, hi)

    for s in range(1, NZ):
        send(own_v, at(0, rels, j), 0, z, zs[s] * 2 + y, n)
    spread(own_v, j, z)
    pltpu.make_async_copy(own_v, at(0, rels, j), out_sem).start()
    k_of = lax.broadcasted_iota(jnp.int32, (rels, q, lanes), 0)
    r_of = lax.broadcasted_iota(jnp.int32, (rels, q, lanes), 1)
    lane = lax.broadcasted_iota(jnp.int32, (rels, q, lanes), 2)
    there = lane == ((k_of + j) * q + r_of) % lanes
    accb[j] = jnp.sum(jnp.sum(jnp.where(there, acc, 0.0), axis=0), axis=0, keepdims=True)
    for p in peers:
        rcopy(accb.at[j], accb.at[j], c_send, c_recv, *peer(*p))

    take(far_l, q_recv.at[3])
    new_left, new_lacc = row_step(wl[n], lacc[...], glb[own, :] + near_l[x] + far_l[...])
    left_v[0] = new_left
    lacc_v[...] = new_lacc
    results = [
        pltpu.make_async_copy(src, dst, res_sem.at[k])
        for k, (src, dst) in enumerate(
            [
                (left_v, left_out),
                (lacc_v, lacc_out),
                (part_r.at[0:rows], right_out.at[0]),
                (racc_v, racc_out),
                (opacc_v, opacc_out),
            ]
        )
    ]
    results[0].start()
    results[1].start()

    for s in range(1, NZ):
        i = shard(zs[s], y, x)
        take(at(0, rels, i), a_recv.at[zs[s]])
        spread(at(0, rels, i), i, zs[s])
        pass_on(zs[s - 1])
        if s > 1:
            last(zs[s - 2], 3, y)
        if s > 2:
            last(zs[s - 3], 5, 1 - y)
    pass_on(zs[NZ - 1])
    take(accb.at[0 : devices - 1], c_recv)
    groups = lanes // q
    rest = jnp.concatenate([accb[i] for i in range(devices)], axis=0)
    diag = lax.broadcasted_iota(jnp.int32, (devices, lanes), 1) // q == (
        lax.broadcasted_iota(jnp.int32, (devices, lanes), 0) % groups
    )
    for k in range(rels):
        turned = rest if k == 0 else pltpu.roll(rest, lanes - k * q, 1)
        turned = jnp.where(diag, turned, 0.0)
        for h in range(devices // groups):
            opacc_v[k : k + 1, h * lanes : (h + 1) * lanes] = jnp.sum(
                turned[h * groups : (h + 1) * groups], axis=0, keepdims=True
            )
    results[4].start()
    moved.wait_recv()
    racc_v[...] = part_r[rows : rows + 1, 0:rows]
    results[2].start()
    results[3].start()
    for s in range(max(NZ - 2, 0), NZ):
        last(zs[s], 3, y)
    for s in range(max(NZ - 3, 0), NZ):
        last(zs[s], 5, 1 - y)
    take(ops_v.at[:, 0 : devices // 2 * q, :], a_recv.at[7 * NZ])
    for cp in results:
        cp.wait()
    pltpu.make_async_copy(own_v, at(0, rels, j), out_sem).wait()
    take(ops_v.at[0:2, 0 : 3 * rows, :], g_send)
    take(ops_v.at[0:2, 0 : 3 * rows, :], q_send)
    take(tagb.at[0 : devices - 1], t_send)
    take(accb.at[0 : devices - 1], c_send)
    take(rsb.at[0 : devices - 1], s_send)
    moved.wait_send()
    take(ops_v.at[:, 0 : (devices - 1) * q, :], a_send)


def write_out(*refs):
    ins, outs, sem = refs[:6], refs[6:12], refs[12]
    moves = [pltpu.make_async_copy(a, b, sem.at[k]) for k, (a, b) in enumerate(zip(ins, outs))]
    moves[4].start()
    for k in (0, 2, 1, 3, 5):
        moves[k].start()
    for cp in moves:
        cp.wait()


def kernel_device(NW, NN, *args):
    left_emb, left_acc, right_emb, right_acc, operators, op_acc = args[:6]
    rows, width = left_emb.shape[1:]
    part = rows * NN
    rels = operators.shape[0]
    devices = NW * NN
    q = operators.shape[1] // devices
    NZ = NW // 2
    left_to_compiler = pl.BlockSpec(memory_space=pl.ANY)
    dma = pltpu.SemaphoreType.DMA
    V = lambda *shape: pltpu.VMEM(shape, F32)
    like = lambda a: pltpu.VMEM(a.shape, a.dtype)
    shapes = [jax.ShapeDtypeStruct(a.shape, a.dtype) for a in args[:6]]
    found = pl.pallas_call(
        functools.partial(kernel, NW, NN),
        out_shape=shapes,
        in_specs=[pl.BlockSpec(memory_space=pltpu.HBM)] * 9
        + [pl.BlockSpec(memory_space=pltpu.SMEM)],
        out_specs=[left_to_compiler] * 6,
        scratch_shapes=[
            like(left_acc),
            like(right_acc),
            like(op_acc),
            like(args[6]),
            like(args[7]),
            like(args[8]),
            like(left_emb),
            like(left_acc),
            like(right_acc),
            like(op_acc),
            V(*operators.shape),
            V(NN, rows, width),
            V(NN, rows, width),
            V(devices, 1, LANES),
            V(devices, 1, LANES),
            V(width, width),
            V(part, width),
            V(part, width),
            V(2, rows, width),
            V(2, rows, width),
            V(rows, width),
            V(rows, width),
            V(rows, width),
            V(rows, width),
            V(devices, q, width),
            V(rows + 8, width),
            V(rows + 8, width),
            V(rels, q, width),
            dma((9,)),
            dma((5,)),
            dma,
            pltpu.SemaphoreType.REGULAR,
            dma,
            dma((6,)),
            dma,
            dma,
            dma,
            dma((NZ,)),
            dma,
            dma((4,)),
            dma,
            dma,
            dma,
            dma,
            dma,
            dma((7 * NZ + 1,)),
        ],
        compiler_params=pltpu.CompilerParams(
            collective_id=0, has_side_effects=True, vmem_limit_bytes=VMEM_LIMIT
        ),
    )(*[pltpu.with_memory_space_constraint(a, pltpu.HBM) for a in args[:9]], args[9])
    return pl.pallas_call(
        write_out,
        out_shape=shapes,
        in_specs=[left_to_compiler] * 6,
        out_specs=[left_to_compiler] * 6,
        scratch_shapes=[dma((6,))],
        compiler_params=pltpu.CompilerParams(vmem_limit_bytes=VMEM_LIMIT),
    )(*found)


def fits(NW, NN, left, ops):
    rows, width = left[1] // NN, left[2]
    devices = NW * NN
    return (
        NN == 4
        and NW >= 4
        and NW & (NW - 1) == 0
        and ops[1] == width
        and ops[1] % (8 * devices) == 0
        and ops[1] // devices == ops[0]
        and ops[1] // NN == rows
        and rows % 8 == 0
        and rows < width
        and width % LANES == 0
        and ops[0] * ops[0] <= LANES
        and LANES % ops[0] == 0
        and devices % (LANES // ops[0]) == 0
    )


def solution(mesh):
    NW, NN = mesh.shape["wide"], mesh.shape["narrow"]
    in_specs = (
        P("wide", "narrow", None),
        P("wide", "narrow"),
        P("wide", "narrow", None),
        P("wide", "narrow"),
        P(),
        P(),
        P("wide", "narrow", None),
        P("wide", "narrow", None),
        P("wide", "narrow", None),
        P("wide", "narrow"),
    )
    out_specs = (
        P("wide", "narrow", None),
        P("wide", "narrow"),
        P("wide", "narrow", None),
        P("wide", "narrow"),
        P(),
        P(),
    )

    def step(*args):
        ok = fits(NW, NN, args[0].shape, args[4].shape)
        body = functools.partial(kernel_device, NW, NN) if ok else plain_device
        return jax.shard_map(
            body, mesh=mesh, in_specs=in_specs, out_specs=out_specs, check_vma=False
        )(*args)

    return step
```

```python
import functools
import jax
import jax.numpy as jnp
from jax import lax
from jax.experimental import pallas as pl
from jax.experimental.pallas import tpu as pltpu
from jax.sharding import PartitionSpec as P

HI = lax.Precision.HIGHEST
MESH = pl.DeviceIdType.MESH
F32 = jnp.float32
BF16 = jnp.bfloat16
VMEM_LIMIT = 32000 * 1024
LANES = 128


def from_behind(value, axis, steps):
    count = lax.axis_size(axis)
    pairs = [(source, (source + steps) % count) for source in range(count)]
    return lax.ppermute(value, axis, pairs)


def group_terms(left_rows, right_rows, neg_rows, rel_op):
    t = jnp.dot(left_rows, rel_op, precision=HI)
    pos = jnp.sum(t * right_rows, axis=-1)
    neg = jnp.dot(t, neg_rows.T, precision=HI)
    gpos = -jax.nn.sigmoid(-pos)
    gneg = jax.nn.sigmoid(neg) / neg_rows.shape[0]
    grad_t = gpos[:, None] * right_rows + jnp.dot(gneg, neg_rows, precision=HI)
    grad_left = jnp.dot(grad_t, rel_op.T, precision=HI)
    grad_right = gpos[:, None] * t
    grad_neg = jnp.dot(gneg.T, t, precision=HI)
    grad_op = jnp.dot(left_rows.T, grad_t, precision=HI)
    return (grad_left, grad_right, grad_neg, grad_op)


def adagrad(param, accum, grad):
    accum_new = accum + jnp.mean(grad * grad, axis=-1)
    return (param - 0.1 * grad / (jnp.sqrt(accum_new)[..., None] + 1e-08), accum_new)


def rows_within(terms, ids, count):
    inside = (ids >= 0) & (ids < count)
    target = jnp.where(inside, ids, count)
    return jax.ops.segment_sum(terms, target, num_segments=count + 1)[:count]


def plain_device(
    left_emb,
    left_acc,
    right_emb,
    right_acc,
    operators,
    op_acc,
    edge_left,
    edge_right,
    negatives,
    group_relation,
):
    whole_left, whole_right = (
        lax.all_gather(left_emb, "narrow", axis=1, tiled=True),
        lax.all_gather(right_emb, "narrow", axis=1, tiled=True),
    )
    lid = edge_left[0, 0]
    rid = edge_right[0, 0]
    nid = negatives[0, 0]
    rel = group_relation[0, 0]
    rel_op = lax.dynamic_index_in_dim(operators, rel, 0, keepdims=False)
    dl, dr, dq, dm = group_terms(
        jnp.take(whole_left[0], lid, axis=0),
        jnp.take(whole_right[0], rid, axis=0),
        jnp.take(whole_right[0], nid, axis=0),
        rel_op,
    )
    right_ids = jnp.concatenate([rid, nid], 0)
    right_terms = jnp.concatenate([dr, dq], 0)
    rows = left_emb.shape[1]
    width = left_emb.shape[2]
    grads = lax.psum_scatter(
        jnp.concatenate(
            [
                rows_within(dl, lid, lax.axis_size("narrow") * rows),
                rows_within(right_terms, right_ids, lax.axis_size("narrow") * rows),
            ],
            1,
        ),
        "narrow",
        scatter_dimension=0,
        tiled=True,
    )
    new_left, new_lacc = adagrad(left_emb[0], left_acc[0], grads[:, :width])
    new_right, new_racc = adagrad(right_emb[0], right_acc[0], grads[:, width:])
    pick = (jnp.arange(operators.shape[0], dtype=jnp.int32) == rel).astype(jnp.float32)
    op_term = pick[:, None, None] * dm[None]
    op_total = lax.psum(op_term, ("wide", "narrow"))
    ops_new, opacc_new = adagrad(operators, op_acc, op_total)
    moved_right, moved_racc = from_behind((new_right, new_racc), "wide", lax.axis_size("wide") // 2)
    return (new_left[None], new_lacc[None], moved_right[None], moved_racc[None], ops_new, opacc_new)


def flip(index, d):
    out = 0
    bit = 1
    total = 0
    while bit <= d:
        here = (index // bit) % 2
        if d & bit:
            out = out + (1 - here) * bit
        else:
            out = out + here * bit
        total += bit
        bit *= 2
    return (index // bit) * bit + out if d else index


def halves(a):
    hi = a.astype(BF16)
    return hi, (a - hi.astype(F32)).astype(BF16)


def dot3(a, b, rhs_t=False):
    (ah, al), (bh, bl) = a, b
    dims = (((1,), (1 if rhs_t else 0,)), ((), ()))
    f = lambda u, v: lax.dot_general(u, v, dims, preferred_element_type=F32)
    return f(ah, bh) + (f(ah, bl) + f(al, bh))


def to_column(row):
    n = row.shape[1]
    eye = lax.broadcasted_iota(jnp.int32, (n, n), 0) == lax.broadcasted_iota(jnp.int32, (n, n), 1)
    return jnp.sum(jnp.where(eye, row, 0.0), axis=1, keepdims=True)


def to_row(column):
    n = column.shape[0]
    eye = lax.broadcasted_iota(jnp.int32, (n, n), 0) == lax.broadcasted_iota(jnp.int32, (n, n), 1)
    return jnp.sum(jnp.where(eye, column, 0.0), axis=0, keepdims=True)


def kernel(
    NW,
    NN,
    left,
    lacc_hbm,
    right,
    racc_hbm,
    ops_hbm,
    opacc_hbm,
    lids_hbm,
    rids_hbm,
    nids_hbm,
    rel_ref,
    left_out,
    lacc_out,
    right_out,
    racc_out,
    ops_out,
    opacc_out,
    lacc,
    racc,
    opacc,
    lids,
    rids,
    nids,
    left_v,
    lacc_v,
    racc_v,
    opacc_v,
    ops_v,
    wl,
    wr,
    tagb,
    accb,
    dm,
    glb,
    grb,
    near_l,
    near_r,
    far_ls,
    far_rs,
    far_l,
    far_r,
    rsb,
    part_s,
    part_r,
    own_v,
    in_sem,
    res_sem,
    out_sem,
    here_sem,
    g_send,
    g_recv,
    t_send,
    t_recv,
    s_send,
    s_recv,
    q_send,
    q_recv,
    p_send,
    p_recv,
    c_send,
    c_recv,
    a_send,
    a_recv,
):
    rows, width = left.shape[1], left.shape[2]
    part = NN * rows
    rels = ops_v.shape[0]
    q = own_v.shape[1]
    hr = rels // 2
    NZ = NW // 2
    devices = NW * NN
    lanes = accb.shape[2]
    w = lax.axis_index("wide")
    n = lax.axis_index("narrow")
    z, y = w // 2, w % 2
    x, c = n // 2, n % 2
    j = n * NW + w
    near, far = flip(n, 1), flip(n, 2)

    def rcopy(src, dst, ss, rs, to_w, to_n):
        cp = pltpu.make_async_remote_copy(
            src_ref=src,
            dst_ref=dst,
            send_sem=ss,
            recv_sem=rs,
            device_id=(to_w, to_n),
            device_id_type=MESH,
        )
        cp.start()
        return cp

    def take(ref, sem):
        pltpu.make_async_copy(ref, ref, sem).wait()

    loads = {}

    def load(name, src, dst):
        cp = pltpu.make_async_copy(src, dst, in_sem.at[len(loads)])
        cp.start()
        loads[name] = cp

    load("l", lids_hbm, lids)
    load("r", rids_hbm, rids)
    load("n", nids_hbm, nids)
    load("left", left.at[0], wl.at[n])
    load("right", right.at[0], wr.at[n])
    load("lacc", lacc_hbm, lacc)
    load("racc", racc_hbm, racc)
    load("opacc", opacc_hbm, opacc)
    load("ops", ops_hbm, ops_v)

    barrier = pltpu.get_barrier_semaphore()
    for d in range(1, NN):
        pl.semaphore_signal(barrier, inc=1, device_id=(w, flip(n, d)), device_id_type=MESH)
    for d in range(1, NW):
        pl.semaphore_signal(barrier, inc=1, device_id=(flip(w, d), n), device_id_type=MESH)
    pl.semaphore_wait(barrier, NN + NW - 2)

    rcopy(left.at[0], wl.at[n], g_send, g_recv.at[0], w, far)
    rcopy(right.at[0], wr.at[n], g_send, g_recv.at[1], w, far)
    rcopy(left.at[0], wl.at[n], g_send, g_recv.at[2], w, near)
    rcopy(right.at[0], wr.at[n], g_send, g_recv.at[3], w, near)
    for d in range(1, NN):
        pl.semaphore_signal(here_sem, inc=1, device_id=(w, flip(n, d)), device_id_type=MESH)

    for name in "lrn":
        loads[name].wait()
    edges, negs = lids.shape[2], nids.shape[2]
    ohl = lax.broadcasted_iota(jnp.int32, (part, edges), 0) == lids[0]
    ohr = lax.broadcasted_iota(jnp.int32, (part, edges), 0) == rids[0]
    ohn = lax.broadcasted_iota(jnp.int32, (part, negs), 0) == nids[0]
    nt = (((1,), (1,)), ((), ()))
    ohl16 = jnp.where(ohl, 1.0, 0.0).astype(BF16)
    ohr16 = jnp.where(ohr, 1.0, 0.0).astype(BF16)
    ohn16 = jnp.where(ohn, 1.0, 0.0).astype(BF16)
    pairs = lax.dot_general(ohl16, ohr16, nt, preferred_element_type=F32)
    cl = jnp.sum(jnp.where(ohl, 1.0, 0.0), axis=1, keepdims=True)
    cn = lax.dot_general(jnp.ones((8, negs), BF16), ohn16, nt, preferred_element_type=F32)[0:1]
    weight = cl * cn

    loads["ops"].wait()
    rel = rel_ref[0, 0]
    m = halves(ops_v[rel])
    tagb[j] = jnp.broadcast_to(rel.astype(F32), tagb.shape[1:])
    pl.semaphore_wait(here_sem, NN - 1)

    order = list(range(NZ - 1, 0, -1)) + [0]
    peers = [
        (dz, dy, dn)
        for dz in order
        for dn in range(NN - 1, -1, -1)
        for dy in (1, 0)
        if dz or dy or dn
    ]

    def peer(dz, dy, dn):
        return flip(z, dz) * 2 + flip(y, dy), flip(n, dn)

    for p in peers:
        rcopy(tagb.at[j], tagb.at[j], t_send, t_recv, *peer(*p))

    take(wl.at[n], g_recv.at[0])
    rcopy(wl.at[far], wl.at[far], g_send, g_recv.at[4], w, near)
    take(wr.at[n], g_recv.at[1])
    rcopy(wr.at[far], wr.at[far], g_send, g_recv.at[5], w, near)
    loads["left"].wait()
    loads["right"].wait()
    take(wl.at[n], g_recv.at[2])
    take(wl.at[n], g_recv.at[4])
    wl_all = wl[...].reshape(part, width)
    t = dot3(halves(wl_all), m)
    th = halves(t)
    wlt = halves(wl_all.T)
    take(wr.at[n], g_recv.at[3])
    take(wr.at[n], g_recv.at[5])
    wrh = halves(wr[...].reshape(part, width))
    s = dot3(th, wrh, rhs_t=True)
    g = weight * (jax.nn.sigmoid(s) / negs) - pairs * jax.nn.sigmoid(-s)
    dt = halves(dot3(halves(g), wrh))
    dm[...] = dot3(wlt, dt)

    def slot(i, size):
        return pl.ds(pl.multiple_of(i * size, size), size)

    for dz, dy, dn in peers:
        to_w, to_n = peer(dz, dy, dn)
        rcopy(dm.at[slot(to_n * NW + to_w, q)], rsb.at[j], s_send, s_recv.at[dz], to_w, to_n)
    rsb[j] = dm[slot(j, q), :]

    grb[...] = dot3(halves(g.T), th)
    for k in range(2):
        rcopy(grb.at[slot(k * 2 + 1 - c, rows)], near_r.at[k], q_send, q_recv.at[0], w, near)
    glb[...] = dot3(dt, m, rhs_t=True)
    for k in range(2):
        rcopy(glb.at[slot(k * 2 + 1 - c, rows)], near_l.at[k], q_send, q_recv.at[1], w, near)

    take(near_r, q_recv.at[0])
    far_rs[...] = grb[slot((1 - x) * 2 + c, rows), :] + near_r[1 - x]
    rcopy(far_rs, far_r, q_send, q_recv.at[2], w, far)
    take(near_l, q_recv.at[1])
    far_ls[...] = glb[slot((1 - x) * 2 + c, rows), :] + near_l[1 - x]
    rcopy(far_ls, far_l, q_send, q_recv.at[3], w, far)

    def row_step(p, acc_row, grad):
        acc = to_column(acc_row) + jnp.sum(grad * grad, axis=1, keepdims=True) / width
        return p - 0.1 * grad / (jnp.sqrt(acc) + 1e-08), to_row(acc)

    own = slot(n, rows)
    for name in ("lacc", "racc", "opacc"):
        loads[name].wait()
    place = lax.broadcasted_iota(jnp.int32, (rels, q, width), 2) == (
        j * q + lax.broadcasted_iota(jnp.int32, (rels, q, width), 1)
    )
    old = jnp.sum(jnp.where(place, opacc[...][:, None, :], 0.0), axis=2, keepdims=True)

    take(tagb.at[0 : devices - 1], t_recv)

    def add_up(dz, total):
        for dn in range(NN):
            for dy in range(2):
                src_w, src_n = peer(dz, dy, dn)
                i = src_n * NW + src_w
                tag = jnp.broadcast_to(tagb[i], (q, lanes))
                tag = jnp.concatenate([tag] * (width // lanes), axis=1)
                term = rsb[i]
                total = [t + jnp.where(tag == k, term, 0.0) for k, t in enumerate(total)]
        return total

    total = [jnp.zeros((q, width), F32) for k in range(rels)]
    take(rsb.at[0 : 2 * NN - 1], s_recv.at[0])
    total = add_up(0, total)
    take(rsb.at[0 : 2 * NN], s_recv.at[1])
    total = add_up(1, total)
    take(far_r, q_recv.at[2])
    new_right, new_racc = row_step(wr[n], racc[...], grb[own, :] + near_r[x] + far_r[...])
    part_s[0:rows, :] = new_right
    part_s[rows : rows + 8, 0:rows] = jnp.broadcast_to(new_racc, (8, rows))
    part_s[rows : rows + 8, rows:width] = jnp.zeros((8, width - rows), F32)
    for dz in range(2, NZ):
        take(rsb.at[0 : 2 * NN], s_recv.at[dz])
        total = add_up(dz, total)

    gop = jnp.stack(total)
    acc = old + jnp.sum(gop * gop, axis=2, keepdims=True) / width
    own_v[...] = ops_v[:, slot(j, q), :] - 0.1 * gop / (jnp.sqrt(acc) + 1e-08)

    def at(r0, r1, i):
        return ops_out.at[r0:r1, slot(i, q), :]

    def shard(zs, ys, xs):
        return (xs * 2 + c) * NW + zs * 2 + ys

    def away(s):
        top = z // (NZ // 2)
        m_z = top * (NZ - 1 - z) + (1 - top) * z
        v = s + (s - m_z + NZ) // NZ
        return top * (NZ - 1 - v) + (1 - top) * v

    wy = z * 2 + (1 - y)
    zs = [z] + [away(s) for s in range(NZ - 1)]

    def send(src, dst, kind, z_of, to_w, to_n):
        rcopy(src, dst, a_send, a_recv.at[kind * NZ + z_of], to_w, to_n)

    def give(src, dst):
        rcopy(src, dst, a_send, a_recv.at[7 * NZ], w, near)

    def spread(src, i, z_of):
        lo, hi = at(0, hr, i), at(hr, rels, i)
        send(src.at[0:hr], lo, 1, z_of, wy, n)
        send(src.at[hr:rels], hi, 2, z_of, w, far)
        send(src.at[0:hr], lo, 3, z_of, w, far)
        send(src.at[hr:rels], hi, 4, z_of, wy, n)
        give(src, at(0, rels, i))

    def pass_on(z_of):
        lo = at(0, hr, shard(z_of, 1 - y, x))
        take(lo, a_recv.at[1 * NZ + z_of])
        send(lo, lo, 5, z_of, w, far)
        give(lo, lo)
        hi = at(hr, rels, shard(z_of, y, 1 - x))
        take(hi, a_recv.at[2 * NZ + z_of])
        send(hi, hi, 6, z_of, wy, n)
        give(hi, hi)

    def last(z_of, kind, lo_y):
        lo = at(0, hr, shard(z_of, lo_y, 1 - x))
        take(lo, a_recv.at[kind * NZ + z_of])
        give(lo, lo)
        hi = at(hr, rels, shard(z_of, 1 - y, x if kind == 3 else 1 - x))
        take(hi, a_recv.at[(kind + 1) * NZ + z_of])
        give(hi, hi)

    for s in range(1, NZ):
        send(own_v, at(0, rels, j), 0, z, zs[s] * 2 + y, n)
    spread(own_v, j, z)
    pltpu.make_async_copy(own_v, at(0, rels, j), out_sem).start()
    k_of = lax.broadcasted_iota(jnp.int32, (rels, q, lanes), 0)
    r_of = lax.broadcasted_iota(jnp.int32, (rels, q, lanes), 1)
    lane = lax.broadcasted_iota(jnp.int32, (rels, q, lanes), 2)
    there = lane == ((k_of + j) * q + r_of) % lanes
    accb[j] = jnp.sum(jnp.sum(jnp.where(there, acc, 0.0), axis=0), axis=0, keepdims=True)
    for p in peers:
        rcopy(accb.at[j], accb.at[j], c_send, c_recv, *peer(*p))

    take(far_l, q_recv.at[3])
    new_left, new_lacc = row_step(wl[n], lacc[...], glb[own, :] + near_l[x] + far_l[...])
    left_v[0] = new_left
    lacc_v[...] = new_lacc
    results = [
        pltpu.make_async_copy(src, dst, res_sem.at[k])
        for k, (src, dst) in enumerate(
            [
                (left_v, left_out),
                (lacc_v, lacc_out),
                (part_r.at[0:rows], right_out.at[0]),
                (racc_v, racc_out),
                (opacc_v, opacc_out),
            ]
        )
    ]
    results[0].start()
    results[1].start()

    for s in range(1, NZ):
        i = shard(zs[s], y, x)
        take(at(0, rels, i), a_recv.at[zs[s]])
        spread(at(0, rels, i), i, zs[s])
        if s == NZ - 1:
            moved = rcopy(part_s, part_r, p_send, p_recv, (w + NW // 2) % NW, n)
        pass_on(zs[s - 1])
        if s > 1:
            last(zs[s - 2], 3, y)
        if s > 2:
            last(zs[s - 3], 5, 1 - y)
    pass_on(zs[NZ - 1])
    take(accb.at[0 : devices - 1], c_recv)
    groups = lanes // q
    rest = jnp.concatenate([accb[i] for i in range(devices)], axis=0)
    diag = lax.broadcasted_iota(jnp.int32, (devices, lanes), 1) // q == (
        lax.broadcasted_iota(jnp.int32, (devices, lanes), 0) % groups
    )
    for k in range(rels):
        turned = rest if k == 0 else pltpu.roll(rest, lanes - k * q, 1)
        turned = jnp.where(diag, turned, 0.0)
        for h in range(devices // groups):
            opacc_v[k : k + 1, h * lanes : (h + 1) * lanes] = jnp.sum(
                turned[h * groups : (h + 1) * groups], axis=0, keepdims=True
            )
    results[4].start()
    for s in range(max(NZ - 2, 0), NZ):
        last(zs[s], 3, y)
    for s in range(max(NZ - 3, 0), NZ):
        last(zs[s], 5, 1 - y)
    moved.wait_recv()
    racc_v[...] = part_r[rows : rows + 1, 0:rows]
    results[2].start()
    results[3].start()
    take(ops_v.at[:, 0 : devices // 2 * q, :], a_recv.at[7 * NZ])
    for cp in results:
        cp.wait()
    pltpu.make_async_copy(own_v, at(0, rels, j), out_sem).wait()
    take(ops_v.at[0:2, 0 : 3 * rows, :], g_send)
    take(ops_v.at[0:2, 0 : 3 * rows, :], q_send)
    take(tagb.at[0 : devices - 1], t_send)
    take(accb.at[0 : devices - 1], c_send)
    take(rsb.at[0 : devices - 1], s_send)
    moved.wait_send()
    take(ops_v.at[:, 0 : (devices - 1) * q, :], a_send)


def write_out(*refs):
    ins, outs, sem = refs[:6], refs[6:12], refs[12]
    moves = [pltpu.make_async_copy(a, b, sem.at[k]) for k, (a, b) in enumerate(zip(ins, outs))]
    moves[4].start()
    for k in (0, 2, 1, 3, 5):
        moves[k].start()
    for cp in moves:
        cp.wait()


def kernel_device(NW, NN, *args):
    left_emb, left_acc, right_emb, right_acc, operators, op_acc = args[:6]
    rows, width = left_emb.shape[1:]
    part = rows * NN
    rels = operators.shape[0]
    devices = NW * NN
    q = operators.shape[1] // devices
    NZ = NW // 2
    left_to_compiler = pl.BlockSpec(memory_space=pl.ANY)
    dma = pltpu.SemaphoreType.DMA
    V = lambda *shape: pltpu.VMEM(shape, F32)
    like = lambda a: pltpu.VMEM(a.shape, a.dtype)
    shapes = [jax.ShapeDtypeStruct(a.shape, a.dtype) for a in args[:6]]
    found = pl.pallas_call(
        functools.partial(kernel, NW, NN),
        out_shape=shapes,
        in_specs=[pl.BlockSpec(memory_space=pltpu.HBM)] * 9
        + [pl.BlockSpec(memory_space=pltpu.SMEM)],
        out_specs=[left_to_compiler] * 6,
        scratch_shapes=[
            like(left_acc),
            like(right_acc),
            like(op_acc),
            like(args[6]),
            like(args[7]),
            like(args[8]),
            like(left_emb),
            like(left_acc),
            like(right_acc),
            like(op_acc),
            V(*operators.shape),
            V(NN, rows, width),
            V(NN, rows, width),
            V(devices, 1, LANES),
            V(devices, 1, LANES),
            V(width, width),
            V(part, width),
            V(part, width),
            V(2, rows, width),
            V(2, rows, width),
            V(rows, width),
            V(rows, width),
            V(rows, width),
            V(rows, width),
            V(devices, q, width),
            V(rows + 8, width),
            V(rows + 8, width),
            V(rels, q, width),
            dma((9,)),
            dma((5,)),
            dma,
            pltpu.SemaphoreType.REGULAR,
            dma,
            dma((6,)),
            dma,
            dma,
            dma,
            dma((NZ,)),
            dma,
            dma((4,)),
            dma,
            dma,
            dma,
            dma,
            dma,
            dma((7 * NZ + 1,)),
        ],
        compiler_params=pltpu.CompilerParams(
            collective_id=0, has_side_effects=True, vmem_limit_bytes=VMEM_LIMIT
        ),
    )(*[pltpu.with_memory_space_constraint(a, pltpu.HBM) for a in args[:9]], args[9])
    return pl.pallas_call(
        write_out,
        out_shape=shapes,
        in_specs=[left_to_compiler] * 6,
        out_specs=[left_to_compiler] * 6,
        scratch_shapes=[dma((6,))],
        compiler_params=pltpu.CompilerParams(vmem_limit_bytes=VMEM_LIMIT),
    )(*found)


def fits(NW, NN, left, ops):
    rows, width = left[1] // NN, left[2]
    devices = NW * NN
    return (
        NN == 4
        and NW >= 4
        and NW & (NW - 1) == 0
        and ops[1] == width
        and ops[1] % (8 * devices) == 0
        and ops[1] // devices == ops[0]
        and ops[1] // NN == rows
        and rows % 8 == 0
        and rows < width
        and width % LANES == 0
        and ops[0] * ops[0] <= LANES
        and LANES % ops[0] == 0
        and devices % (LANES // ops[0]) == 0
    )


def solution(mesh):
    NW, NN = mesh.shape["wide"], mesh.shape["narrow"]
    in_specs = (
        P("wide", "narrow", None),
        P("wide", "narrow"),
        P("wide", "narrow", None),
        P("wide", "narrow"),
        P(),
        P(),
        P("wide", "narrow", None),
        P("wide", "narrow", None),
        P("wide", "narrow", None),
        P("wide", "narrow"),
    )
    out_specs = (
        P("wide", "narrow", None),
        P("wide", "narrow"),
        P("wide", "narrow", None),
        P("wide", "narrow"),
        P(),
        P(),
    )

    def step(*args):
        ok = fits(NW, NN, args[0].shape, args[4].shape)
        body = functools.partial(kernel_device, NW, NN) if ok else plain_device
        return jax.shard_map(
            body, mesh=mesh, in_specs=in_specs, out_specs=out_specs, check_vma=False
        )(*args)

    return step
```
